128 devices in a mesh: row: 8 (over z, x_lo), col: 16 (over y, x_hi, core).
Axes of the slice: x: 4 (x_hi: 2, x_lo: 2; x = x_hi * 2 + x_lo), y: 4, z: 4, core: 2. Of those that a mesh axis runs over, the one named last changes fastest.
Arguments:
- tokens: bfloat16 [1024, 12288], P('col', 'row'), may hold values from -6 to 6
- out_grad: bfloat16 [1024, 49152], P('row', 'col'), may hold values from -6 to 6
- weight: bfloat16 [12288, 49152], P('row', 'col'), may hold values from -0.09375 to 0.09375
- block_mask: int32 [48, 192], P('row', 'col'), may hold values 0 or 1
Outputs:
- input_grad: bfloat16 [1024, 12288], P('col', 'row')
- weight_grad: bfloat16 [12288, 49152], P('row', 'col')
The draws below stay inside these ranges and needn't reach their ends.
All inputs are finite; a program needn't handle non-finite values. No bound on the sum of `block_mask` on one device may be relied on, other than what follows from the above.
Results may differ from the reference program's by a relative error of at most 0.015.
Values may be sent and summed in bfloat16 or wider, within the bound.
A program may use at most 192 MiB of HBM per device.

```python
import jax
import jax.numpy as jnp
from jax import lax

D = 12288
FF = 49152
BLOCK = 256
TOKENS = 1024
N_COL = 16


def set_ends(array, key, low, top_value):
    spot = [jax.random.randint(jax.random.fold_in(key, axis), (), 0, length) for axis, length in enumerate(array.shape)]
    longest = array.shape.index(max(array.shape))
    neighbour = spot[:longest] + [(spot[longest] + 1) % array.shape[longest]] + spot[longest + 1:]
    return array.at[tuple(spot)].set(low).at[tuple(neighbour)].set(top_value)


def with_spikes(result, key, source, target, blocks, factor):
    def block_of(position):
        return (jnp.arange(result.shape[position]) // (result.shape[position] // blocks)).reshape((-1,) + (1,) * (result.ndim - 1 - position))

    first = jax.random.permutation(key, blocks)[block_of(target)]
    far = (block_of(target) + blocks // 2) % blocks
    return jnp.where((block_of(source) == first) | (block_of(source) == far), factor * result, result)


def level_of(rng, extent, split, low, largest):
    def one(dim, parts):
        heights = jax.random.uniform(jax.random.fold_in(jax.random.fold_in(rng, 6), dim), (parts,), jnp.float32, low / len(split), largest / len(split))
        return jnp.repeat(jnp.exp(heights), extent[dim] // parts).reshape((-1,) + (1,) * (len(extent) - dim - 1))

    gain = one(*split[0])
    for cut in split[1:]:
        gain = gain * one(*cut)
    return gain


def scatter_about(key, shape, deviation, bound, split=(), kind=jnp.bfloat16):
    result = jax.random.normal(key, shape, jnp.float32) * deviation
    if len(split) > 0:
        result = level_of(key, shape, split, -0.22, 0.18) * result
    return jnp.clip(result, min=-bound, max=bound).astype(kind)


def gaussian_with(stream_key, dims, spread, most, pieces, heavy, kind=jnp.bfloat16):
    values = spread * jax.random.normal(stream_key, dims, jnp.float32)
    if pieces:
        values = values * level_of(stream_key, dims, pieces, -0.22, 0.18)
    return jnp.clip(with_spikes(values, jax.random.fold_in(stream_key, 3), *heavy), -most, most).astype(kind)


def setup_inputs(seed: int = 0) -> dict:
    key_of = jax.random.split(jax.random.key(seed), 5)
    tokens = scatter_about(key_of[0], (TOKENS, D), 1.0, 6.0, ((0, 16), (1, 8)))
    out_grad = gaussian_with(key_of[1], (TOKENS, FF), 1.0, 6.0, ((0, 8), (1, 16)), (1, 0, 16, 2.0))
    weight = scatter_about(key_of[2], (D, FF), (3 * D // 10) ** -0.5, 0.09375, ((0, 8), (1, 16)))
    block_mask = set_ends((jax.random.randint(key_of[3], (D // BLOCK, FF // BLOCK), 0, 10) < 3).astype(jnp.int32), jax.random.fold_in(key_of[3], 1), 0, 1)
    return {"tokens": tokens, "out_grad": out_grad, "weight": weight, "block_mask": block_mask}


def reference(tokens, out_grad, weight, block_mask):
    keep_blocks = block_mask.astype(jnp.float32)
    width = FF // N_COL
    block_cols = width // BLOCK
    block_rows = D // BLOCK

    def one_group(accum, group_index):
        offset = (group_index * width).astype(jnp.int32)
        weight_panel = lax.dynamic_slice_in_dim(weight, offset, width, 1).astype(jnp.float32)
        keep_panel = lax.dynamic_slice_in_dim(keep_blocks, (group_index * block_cols).astype(jnp.int32), block_cols, 1)
        masked = (weight_panel.reshape(block_rows, BLOCK, block_cols, BLOCK) * keep_panel[:, None, :, None]).reshape(D, width).astype(jnp.bfloat16)
        grad_panel = lax.dynamic_slice_in_dim(out_grad, offset, width, 1)
        partial_value = lax.dot_general(grad_panel, masked, (((1,), (1,)), ((), ())), preferred_element_type=jnp.float32)
        accum = accum + partial_value.astype(jnp.bfloat16).astype(jnp.float32)
        full_grad = lax.dot_general(tokens, grad_panel, (((0,), (0,)), ((), ())), preferred_element_type=jnp.float32)
        kept_grad = (full_grad.reshape(block_rows, BLOCK, block_cols, BLOCK) * keep_panel[:, None, :, None]).reshape(D, width)
        return accum, kept_grad.astype(jnp.bfloat16)

    start_sum = jnp.zeros((tokens.shape[0], D), jnp.float32)
    accum, grads = lax.scan(one_group, start_sum, jnp.arange(N_COL, dtype=jnp.int32))
    weight_grad = jnp.transpose(grads, (1, 0, 2)).reshape(D, FF)
    return accum.astype(jnp.bfloat16), weight_grad
```

```python
import functools

import jax
import jax.numpy as jnp
from jax import lax
from jax.experimental import pallas as pl
from jax.experimental.pallas import tpu as pltpu
from jax.sharding import PartitionSpec as P

BLOCK = 256
MESH = pl.DeviceIdType.MESH
BF = jnp.bfloat16
F32 = jnp.float32

SHARDS = ((0, 0), (1, 0), (3, 0), (0, 1), (2, 0), (1, 1), (3, 1), (2, 1))
ZP, ZM, XN, RP, RM, BP, BM, XX = 0, 2, 4, 6, 7, 8, 10, 12
TX, TYP, TYM, TRP, TRM = 0, 1, 3, 5, 6


def gather_kernel(
    mask, tok, og, w, ig_out, g_out, tt_out,
    gbuf, tbuf, wbuf, ttbuf, pbuf, cbuf, sbuf, ybuf, xbuf, fbuf, obuf,
    gsend, grecv, tsend, trecv, tcsend, tcrecv, csend, crecv, ysend, yrecv, xsend, xrecv,
    wsem, lsem, gosem, tosem, iosem,
):
    row, col = lax.axis_index("row"), lax.axis_index("col")
    z, p = lax.div(row, 2), lax.rem(row, 2)
    y, q, k = lax.div(col, 4), lax.rem(lax.div(col, 2), 2), lax.rem(col, 2)

    def ring(v, step):
        return lax.rem(v + step, 4)

    def device(z_=z, p_=p, y_=y, q_=q, k_=k):
        return (2 * z_ + p_, 4 * y_ + 2 * q_ + k_)

    z_up, z_down = device(z_=ring(z, 1)), device(z_=ring(z, 3))
    x_near = device(p_=1 - p)
    y_up, y_down = device(y_=ring(y, 1)), device(y_=ring(y, 3))
    x_far, other = device(q_=1 - q), device(k_=1 - k)

    def remote(src, dst, send, recv, to):
        return pltpu.make_async_remote_copy(
            src_ref=src, dst_ref=dst, send_sem=send, recv_sem=recv, device_id=to, device_id_type=MESH
        )

    def piece(dz, pp, h):
        p_ = 1 - p if pp else p
        return gbuf.at[pl.ds(4 * ring(z, dz) + 2 * p_, 2), pl.ds(32 * h, 32), :]

    def g_send(kind, h, dz, pp, to, src=None):
        ref = piece(dz, pp, h)
        remote(ref if src is None else src, ref, gsend.at[kind], grecv.at[kind], to).start()

    def g_wait(kind, h, dz, pp):
        ref = piece(dz, pp, h)
        remote(ref, ref, gsend.at[kind], grecv.at[kind], z_up).wait_recv()

    def t_slot(dy, qq, k_=k):
        q_ = 1 - q if qq else q
        return tbuf.at[4 * ring(y, dy) + 2 * q_ + k_]

    def t_send(kind, dy, qq, to, src=None):
        ref = t_slot(dy, qq)
        remote(ref if src is None else src, ref, tsend.at[kind], trecv.at[kind], to).start()

    def t_wait(kind, dy, qq):
        ref = t_slot(dy, qq)
        remote(ref, ref, tsend.at[kind], trecv.at[kind], y_up).wait_recv()

    def t_share(dy, qq, src=None):
        ref = t_slot(dy, qq)
        n = 2 * dy + qq
        remote(ref if src is None else src, ref, tcsend.at[n], tcrecv.at[n], other).start()

    blocks = wbuf.shape[0] // BLOCK

    def w_load(i):
        part = pl.ds(i * BLOCK, BLOCK)
        return pltpu.make_async_copy(w.at[part, :], wbuf.at[part, :], wsem.at[i])

    own_g = pltpu.make_async_copy(og, gbuf.at[pl.ds(4 * z + 2 * p, 2)], lsem.at[0])
    own_t = pltpu.make_async_copy(tok, t_slot(0, 0), lsem.at[1])
    own_g.start()
    for i in range(blocks):
        w_load(i).start()
    own_t.start()

    barrier = pltpu.get_barrier_semaphore()
    peers = (z_up, z_down, x_near, y_up, y_down, x_far, other)
    for peer in peers:
        pl.semaphore_signal(barrier, inc=1, device_id=peer, device_id_type=MESH)
    pl.semaphore_wait(barrier, len(peers))

    def half_of_own(h):
        return og.at[:, pl.ds(32 * h, 32), :]

    g_send(ZP + 0, 0, 0, 0, z_up, half_of_own(0))
    g_send(ZM + 1, 1, 0, 0, z_down, half_of_own(1))
    t_send(TX, 0, 0, x_far, tok)
    g_send(XN + 0, 0, 0, 0, x_near, half_of_own(0))
    g_send(ZP + 1, 1, 0, 0, z_up, half_of_own(1))
    g_send(ZM + 0, 0, 0, 0, z_down, half_of_own(0))
    g_send(XN + 1, 1, 0, 0, x_near, half_of_own(1))
    t_send(TYP, 0, 0, y_up, tok)
    t_send(TYM, 0, 0, y_down, tok)
    t_share(0, 0, tok)

    for i in range(blocks):
        w_load(i).wait()
        rows = pl.ds(i * BLOCK, BLOCK)
        for j in range(wbuf.shape[1] // BLOCK):
            cols = pl.ds(j * BLOCK, BLOCK)
            keep = mask[i, j].astype(F32).astype(BF)
            wbuf[rows, cols] = wbuf[rows, cols] * keep

    def partial_sums(shards, halves):
        def step(n, _):
            part = pl.ds(pl.multiple_of(n * BLOCK, BLOCK), BLOCK)
            rhs = wbuf[part, :]
            pieces = []
            for s in shards:
                dz, pp = SHARDS[s]
                p_ = 1 - p if pp else p
                first = 4 * ring(z, dz) + 2 * p_
                if len(halves) == 2:
                    value = gbuf[pl.ds(first, 2), :, :].reshape(128, gbuf.shape[2])
                else:
                    value = gbuf[pl.ds(first, 2), pl.ds(32 * halves[0], 32), :].reshape(64, gbuf.shape[2])
                pieces.append(value)
            lhs = pieces[0] if len(pieces) == 1 else jnp.concatenate(pieces, axis=0)
            out = lax.dot_general(lhs, rhs, (((1,), (1,)), ((), ())), preferred_element_type=F32)
            out = out.astype(BF).reshape(len(shards), 2, len(halves), 32, BLOCK)
            for a, s in enumerate(shards):
                for b, h in enumerate(halves):
                    for c in range(2):
                        pbuf[2 * s + h, c, :, part] = out[a, c, b]
            return 0

        lax.fori_loop(0, blocks, step, 0)

    def core_copy(u):
        return remote(pbuf.at[u, 1 - k], cbuf.at[u], csend.at[u], crecv.at[u], other)

    def source_of(u):
        dz, pp = SHARDS[u // 2]
        p_ = 1 - p if pp else p
        return lax.rem(y + 8 - z - dz, 4), p_

    low, high = pl.ds(0, 16), pl.ds(16, 16)

    def y_copy(u, side, part, number, to):
        return remote(
            sbuf.at[u, part, :], ybuf.at[u, side, part, :], ysend.at[u, number],
            yrecv.at[u, side, 0 if part is low else 1], to,
        )

    def y_wait(u, side, part):
        ref = ybuf.at[u, side, part, :]
        remote(ref, ref, ysend.at[u, 0], yrecv.at[u, side, 0 if part is low else 1], y_up).wait_recv()

    def stage1(u):
        core_copy(u).wait_recv()
        sbuf[u] = (pbuf[u, k].astype(F32) + cbuf[u].astype(F32)).astype(BF)
        away, _ = source_of(u)

        @pl.when(away == 2)
        def _():
            y_copy(u, 0, low, 0, y_up).start()
            y_copy(u, 1, high, 1, y_down).start()

        @pl.when(away == 3)
        def _():
            y_copy(u, 0, high, 0, y_up).start()

        @pl.when(away == 1)
        def _():
            y_copy(u, 1, low, 0, y_down).start()

    def stage2(u):
        away, _ = source_of(u)

        @pl.when(away == 3)
        def _():
            y_wait(u, 0, low)
            sbuf[u, low, :] = (sbuf[u, low, :].astype(F32) + ybuf[u, 0, low, :].astype(F32)).astype(BF)
            y_copy(u, 0, low, 1, y_up).start()

        @pl.when(away == 1)
        def _():
            y_wait(u, 1, high)
            sbuf[u, high, :] = (sbuf[u, high, :].astype(F32) + ybuf[u, 1, high, :].astype(F32)).astype(BF)
            y_copy(u, 1, high, 1, y_down).start()

    def x_copy(h):
        return remote(obuf.at[h], xbuf.at[h], xsend.at[h], xrecv.at[h], x_far)

    def stage3(u):
        away, p_ = source_of(u)
        h = u % 2

        @pl.when(away == 0)
        def _():
            for side in range(2):
                for part in (low, high):
                    y_wait(u, side, part)
            total = sbuf[u].astype(F32) + ybuf[u, 0].astype(F32) + ybuf[u, 1].astype(F32)

            @pl.when(p_ == q)
            def _():
                fbuf[h] = total

            @pl.when(p_ != q)
            def _():
                obuf[h] = total.astype(BF)
                x_copy(h).start()

    def units(*shards):
        return [2 * s + h for s in shards for h in range(2)]

    def g_store(s):
        dz, pp = SHARDS[s]
        p_ = 1 - p if pp else p
        part = pl.ds(4 * ring(z, dz) + 2 * p_, 2)
        return pltpu.make_async_copy(gbuf.at[part], g_out.at[part], gosem.at[s])

    own_g.wait()
    partial_sums((0,), (0, 1))
    for u in units(0):
        core_copy(u).start()
    g_store(0).start()

    t_wait(TX, 0, 1)
    t_send(TYP + 1, 0, 1, y_up)
    t_send(TYM + 1, 0, 1, y_down)
    t_share(0, 1)

    g_wait(ZP + 0, 0, 3, 0)
    g_send(RP, 0, 3, 0, z_up)
    g_wait(ZM + 1, 1, 1, 0)
    g_send(RM, 1, 1, 0, z_down)
    g_wait(XN + 0, 0, 0, 1)
    g_send(BP + 0, 0, 0, 1, z_up)
    g_send(BM + 0, 0, 0, 1, z_down)

    for u in units(0):
        stage1(u)
    t_wait(TYP, 3, 0)
    t_send(TRP, 3, 0, y_up)
    t_share(3, 0)
    t_wait(TYM, 1, 0)
    t_share(1, 0)
    t_wait(TYM + 1, 1, 1)
    t_send(TRM, 1, 1, y_down)
    t_share(1, 1)
    t_wait(TYP + 1, 3, 1)
    t_share(3, 1)

    g_wait(ZP + 1, 1, 3, 0)
    g_wait(ZM + 0, 0, 1, 0)
    g_wait(XN + 1, 1, 0, 1)
    g_send(BP + 1, 1, 0, 1, z_up)
    g_send(BM + 1, 1, 0, 1, z_down)
    partial_sums((1, 2, 3), (0, 1))
    for u in units(1, 2, 3):
        core_copy(u).start()
    for s in (1, 2, 3):
        g_store(s).start()
    for u in units(0):
        stage2(u)

    g_wait(RP, 0, 2, 0)
    g_send(XX + 0, 0, 2, 0, x_near)
    g_wait(RM, 1, 2, 0)
    g_send(XX + 1, 1, 2, 0, x_near)
    for u in units(1, 2, 3):
        stage1(u)
    partial_sums((4,), (0, 1))
    for u in units(4):
        core_copy(u).start()
    g_store(4).start()
    for u in units(0):
        stage3(u)
    for u in units(1, 2, 3):
        stage2(u)
    for u in units(4):
        stage1(u)

    t_wait(TRP, 2, 0)
    t_share(2, 0)
    t_wait(TRM, 2, 1)
    t_share(2, 1)
    own_t.wait()
    for n in range(8):
        ref = t_slot(n // 2, n % 2, 1 - k)
        remote(ref, ref, tcsend.at[n], tcrecv.at[n], other).wait_recv()

    def flip(m, _):
        at = pl.ds(pl.multiple_of(m * 128, 128), 128)
        for i in range(blocks):
            part = pl.ds(i * BLOCK, BLOCK)
            ttbuf[part, at] = tbuf[pl.ds(2 * m, 2), :, part].reshape(128, BLOCK).T
        return 0

    lax.fori_loop(0, 8, flip, 0)
    t_store = pltpu.make_async_copy(ttbuf, tt_out, tosem)
    t_store.start()

    for u in units(1, 2, 3):
        stage3(u)
    for u in units(4):
        stage2(u)

    for h in range(2):
        g_wait(BP + h, h, 3, 1)
        g_wait(BM + h, h, 1, 1)
        g_wait(XX + h, h, 2, 1)
        if h == 1:
            for s in (5, 6, 7):
                g_store(s).start()
        partial_sums((5, 6, 7), (h,))
        late = [2 * s + h for s in (5, 6, 7)]
        for u in late:
            core_copy(u).start()
        if h == 0:
            for u in units(4):
                stage3(u)
        for u in late:
            stage1(u)
        for u in late:
            stage2(u)
        if h == 1:
            for u in (10, 12, 14):
                stage3(u)
    for u in (11, 13, 15):
        stage3(u)

    for h in range(2):
        x_copy(h).wait_recv()
        fbuf[h] = fbuf[h] + xbuf[h].astype(F32)
    for h in range(2):
        x_copy(h).wait_send()
        obuf[h] = fbuf[h].astype(BF)
    i_store = pltpu.make_async_copy(obuf, ig_out, iosem)
    i_store.start()

    for kind in range(14):
        ref = piece(0, 0, 0)
        remote(ref, ref, gsend.at[kind], grecv.at[kind], z_up).wait_send()
    for kind in range(7):
        ref = t_slot(0, 0)
        remote(ref, ref, tsend.at[kind], trecv.at[kind], y_up).wait_send()
    for n in range(8):
        ref = t_slot(0, 0)
        remote(ref, ref, tcsend.at[n], tcrecv.at[n], other).wait_send()
    for u in range(16):
        core_copy(u).wait_send()
        away, _ = source_of(u)

        @pl.when(away != 0)
        def _():
            y_copy(u, 0, low, 0, y_up).wait_send()
            y_copy(u, 0, low, 1, y_up).wait_send()

    for s in range(8):
        g_store(s).wait()
    t_store.wait()
    i_store.wait()


def gather_call(tokens, out_grad, weight, block_mask):
    d, ff = weight.shape
    half, whole, any_ = pltpu.VMEM, pl.BlockSpec(memory_space=pl.ANY), pl.ANY
    dma = pltpu.SemaphoreType.DMA
    return pl.pallas_call(
        gather_kernel,
        out_shape=(
            jax.ShapeDtypeStruct((2, 32, d), BF),
            jax.ShapeDtypeStruct((16, 64, ff), BF),
            jax.ShapeDtypeStruct((d, 1024), BF),
        ),
        in_specs=[pl.BlockSpec(memory_space=pltpu.SMEM), whole, whole, whole],
        out_specs=(whole, whole, whole),
        scratch_shapes=[
            half((16, 64, ff), BF),
            half((16, 64, d), BF),
            half((d, ff), BF),
            half((d, 1024), BF),
            half((16, 2, 32, d), BF),
            half((16, 32, d), BF),
            half((16, 32, d), BF),
            half((16, 2, 32, d), BF),
            half((2, 32, d), BF),
            half((2, 32, d), F32),
            half((2, 32, d), BF),
            dma((14,)), dma((14,)), dma((7,)), dma((7,)), dma((8,)), dma((8,)),
            dma((16,)), dma((16,)), dma((16, 2)), dma((16, 2, 2)), dma((2,)), dma((2,)),
            dma((d // BLOCK,)), dma((2,)), dma((8,)), dma, dma,
        ],
        compiler_params=pltpu.CompilerParams(
            collective_id=0, has_side_effects=True, vmem_limit_bytes=60 * 1024 * 1024
        ),
        name="gather_and_input_grad",
    )(block_mask, tokens, out_grad.reshape(2, 64, ff), weight)


def weight_kernel(mask, ig_in, g, tt, ig_out, wg, igv, gv, ttv, ov, isem, gsem, tsem, osem):
    d, ff = wg.shape
    rows, cols = d // BLOCK, ff // BLOCK

    def strip(j):
        return pl.ds(pl.multiple_of(j * BLOCK, BLOCK), BLOCK)

    def g_load(j):
        return pltpu.make_async_copy(g.at[:, strip(j)], gv.at[:, strip(j)], gsem.at[j])

    t_load = pltpu.make_async_copy(tt, ttv, tsem)
    i_load = pltpu.make_async_copy(ig_in, igv, isem.at[0])
    i_save = pltpu.make_async_copy(igv, ig_out, isem.at[1])
    t_load.start()
    for j in range(cols):
        g_load(j).start()
    i_load.start()

    def save(j):
        return pltpu.make_async_copy(ov.at[j], wg.at[:, strip(j)], osem.at[j])

    t_load.wait()

    def one(j, _):
        g_load(j).wait()
        for i in range(rows):
            part = pl.ds(i * BLOCK, BLOCK)

            @pl.when(mask[i, j] != 0)
            def _():
                ov[j, part, :] = jnp.dot(
                    ttv[part, :], gv[:, strip(j)], preferred_element_type=F32
                ).astype(BF)

            @pl.when(mask[i, j] == 0)
            def _():
                ov[j, part, :] = jnp.zeros((BLOCK, BLOCK), BF)

        save(j).start()
        return 0

    lax.fori_loop(0, cols, one, 0)
    i_load.wait()
    i_save.start()
    for j in range(cols):
        save(j).wait()
    i_save.wait()


def weight_call(block_mask, input_grad, g, tt):
    (d, tokens), ff = tt.shape, g.shape[1]
    whole = pl.BlockSpec(memory_space=pl.ANY)
    dma = pltpu.SemaphoreType.DMA
    return pl.pallas_call(
        weight_kernel,
        out_shape=(jax.ShapeDtypeStruct(input_grad.shape, BF), jax.ShapeDtypeStruct((d, ff), BF)),
        in_specs=[pl.BlockSpec(memory_space=pltpu.SMEM), whole, whole, whole],
        out_specs=(whole, whole),
        scratch_shapes=[
            pltpu.VMEM(input_grad.shape, BF),
            pltpu.VMEM((tokens, ff), BF),
            pltpu.VMEM((d, tokens), BF),
            pltpu.VMEM((ff // BLOCK, d, BLOCK), BF),
            dma((2,)), dma((ff // BLOCK,)), dma, dma((ff // BLOCK,)),
        ],
        compiler_params=pltpu.CompilerParams(vmem_limit_bytes=60 * 1024 * 1024),
        name="weight_grad",
    )(block_mask, input_grad, g, tt)


def local(tokens, out_grad, weight, block_mask):
    d, ff = weight.shape
    ig, g, tt = gather_call(tokens, out_grad, weight, block_mask)
    return weight_call(block_mask, ig.reshape(64, d), g.reshape(1024, ff), tt)


def solution(mesh):
    in_specs = (P("col", "row"), P("row", "col"), P("row", "col"), P("row", "col"))
    out_specs = (P("col", "row"), P("row", "col"))
    return jax.shard_map(local, mesh=mesh, in_specs=in_specs, out_specs=out_specs, check_vma=False)
```

```python
import jax
import jax.numpy as jnp
from jax import lax
from jax.experimental import pallas as pl
from jax.experimental.pallas import tpu as pltpu
from jax.sharding import PartitionSpec as P

BLOCK = 256
MESH = pl.DeviceIdType.MESH
BF = jnp.bfloat16
F32 = jnp.float32

SHARDS = ((0, 0), (1, 0), (3, 0), (0, 1), (3, 1), (2, 0), (1, 1), (2, 1))
LAST = 7
ZP, ZM, XN, XX, RP, RM, BP, BM, CP, CM = 0, 2, 4, 6, 8, 9, 10, 12, 14, 16
G_COPIES = 18
TX, TYP, TYM, TRP, TRM = 0, 1, 3, 5, 6


def main_kernel(
    mask, tok, og, w, ig_out, wg_out,
    gbuf, tbuf, wbuf, wt, tt_early, tt_late, acc, stage, pbuf, cbuf, sbuf, ybuf, xbuf, fbuf, obuf,
    gsend, grecv, tsend, trecv, tcsend, tcrecv, csend, crecv, ysend, yrecv, xsend, xrecv,
    wsem, lsem, osem, iosem,
):
    row, col = lax.axis_index("row"), lax.axis_index("col")
    z, p = lax.div(row, 2), lax.rem(row, 2)
    y, q, k = lax.div(col, 4), lax.rem(lax.div(col, 2), 2), lax.rem(col, 2)

    def ring(v, step):
        return lax.rem(v + step, 4)

    def device(z_=z, p_=p, y_=y, q_=q, k_=k):
        return (2 * z_ + p_, 4 * y_ + 2 * q_ + k_)

    z_up, z_down = device(z_=ring(z, 1)), device(z_=ring(z, 3))
    x_near = device(p_=1 - p)
    y_up, y_down = device(y_=ring(y, 1)), device(y_=ring(y, 3))
    x_far, other = device(q_=1 - q), device(k_=1 - k)

    def remote(src, dst, send, recv, to):
        return pltpu.make_async_remote_copy(
            src_ref=src, dst_ref=dst, send_sem=send, recv_sem=recv, device_id=to, device_id_type=MESH
        )

    def first_of(dz, pp):
        return 4 * ring(z, dz) + 2 * (1 - p if pp else p)

    def piece(dz, pp, start, size=32):
        return gbuf.at[pl.ds(first_of(dz, pp), 2), pl.ds(start, size), :]

    def g_send(kind, start, dz, pp, to, src=None, size=32):
        ref = piece(dz, pp, start, size)
        remote(ref if src is None else src, ref, gsend.at[kind], grecv.at[kind], to).start()

    def g_wait(kind, start, dz, pp, size=32):
        ref = piece(dz, pp, start, size)
        remote(ref, ref, gsend.at[kind], grecv.at[kind], z_up).wait_recv()

    def t_slot(dy, qq, k_=k):
        q_ = 1 - q if qq else q
        return tbuf.at[4 * ring(y, dy) + 2 * q_ + k_]

    def t_send(kind, dy, qq, to, src=None):
        ref = t_slot(dy, qq)
        remote(ref if src is None else src, ref, tsend.at[kind], trecv.at[kind], to).start()

    def t_wait(kind, dy, qq):
        ref = t_slot(dy, qq)
        remote(ref, ref, tsend.at[kind], trecv.at[kind], y_up).wait_recv()

    def t_share(dy, qq, src=None):
        ref = t_slot(dy, qq)
        n = 2 * dy + qq
        remote(ref if src is None else src, ref, tcsend.at[n], tcrecv.at[n], other).start()

    blocks = wt.shape[1] // BLOCK
    strips = wt.shape[0] // BLOCK

    def w_load(i):
        return pltpu.make_async_copy(w.at[pl.ds(i * BLOCK, BLOCK), :], wbuf.at[i % 2], wsem.at[i])

    own_g = pltpu.make_async_copy(og, gbuf.at[pl.ds(4 * z + 2 * p, 2)], lsem.at[0])
    own_t = pltpu.make_async_copy(tok, t_slot(0, 0), lsem.at[1])
    own_g.start()
    w_load(0).start()
    w_load(1).start()
    own_t.start()

    barrier = pltpu.get_barrier_semaphore()
    peers = (z_up, z_down, x_near, y_up, y_down, x_far, other)
    for peer in peers:
        pl.semaphore_signal(barrier, inc=1, device_id=peer, device_id_type=MESH)
    pl.semaphore_wait(barrier, len(peers))

    def half_of_own(h):
        return og.at[:, pl.ds(32 * h, 32), :]

    g_send(ZP + 1, 32, 0, 0, z_up, half_of_own(1))
    g_send(ZM + 1, 32, 0, 0, z_down, half_of_own(1))
    g_send(XN + 0, 0, 0, 0, x_near, half_of_own(0))
    t_send(TX, 0, 0, x_far, tok)
    g_send(ZP + 0, 0, 0, 0, z_up, half_of_own(0))
    g_send(ZM + 0, 0, 0, 0, z_down, half_of_own(0))
    g_send(XN + 1, 32, 0, 0, x_near, half_of_own(1))
    t_send(TYP, 0, 0, y_up, tok)
    t_send(TYM, 0, 0, y_down, tok)
    t_share(0, 0, tok)

    for i in range(blocks):
        w_load(i).wait()

        def turn(j, _, i=i):
            cols = pl.ds(pl.multiple_of(j * BLOCK, BLOCK), BLOCK)
            keep = mask[i, j].astype(F32).astype(BF)
            wt[cols, pl.ds(i * BLOCK, BLOCK)] = (wbuf[i % 2, :, cols] * keep).T
            return 0

        lax.fori_loop(0, strips, turn, 0)
        if i + 2 < blocks:
            w_load(i + 2).start()

    def g_rows(items, part):
        values = []
        for s, halves in items:
            first = first_of(*SHARDS[s])
            if len(halves) == 2:
                value = gbuf[pl.ds(first, 2), :, part]
            elif s < LAST:
                value = gbuf[pl.ds(first, 2), pl.ds(32 * halves[0], 32), part]
            else:
                value = gbuf[pl.ds(first, 2), pl.ds(16 * halves[0], 16), part]
                values.append(value.reshape(32, value.shape[2]))
                value = gbuf[pl.ds(first, 2), pl.ds(16 * halves[0] + 32, 16), part]
            values.append(value.reshape(value.shape[0] * value.shape[1], value.shape[2]))
        return values[0] if len(values) == 1 else jnp.concatenate(values, axis=0)

    def whole_shards(*shards):
        return [(s, (0, 1)) for s in shards]

    def partial_sums(items):
        def step(n, _):
            part = pl.ds(pl.multiple_of(n * BLOCK, BLOCK), BLOCK)
            out = jnp.dot(g_rows(items, slice(None)), wt[:, part], preferred_element_type=F32).astype(BF)
            row = 0
            for s, halves in items:
                if s == LAST:
                    for e in range(2):
                        for c in range(2):
                            pbuf[2 * s + halves[0], c, pl.ds(16 * e, 16), part] = out[row : row + 16]
                            row += 16
                    continue
                for c in range(2):
                    for h in halves:
                        pbuf[2 * s + h, c, :, part] = out[row : row + 32]
                        row += 32
            return 0

        lax.fori_loop(0, blocks, step, 0)
        for s, halves in items:
            for h in halves:
                core_copy(2 * s + h).start()

    def strip_of(n):
        return pl.ds(pl.multiple_of(n * BLOCK, BLOCK), BLOCK)

    def first_pass(n, _):
        acc[n] = jnp.dot(tt_early[...], g_rows(whole_shards(0, 1, 2, 3), strip_of(n)), preferred_element_type=F32)
        return 0

    def w_store(n):
        slot = lax.rem(n, 3)
        return pltpu.make_async_copy(stage.at[slot], wg_out.at[:, strip_of(n)], osem.at[slot])

    def last_pass(n, _):
        @pl.when(n >= 3)
        def _():
            w_store(n - 3).wait()

        total = acc[n] + jnp.dot(
            tt_late[...], g_rows(whole_shards(4, 5, 6, 7), strip_of(n)), preferred_element_type=F32
        )
        stage[lax.rem(n, 3)] = total.astype(BF)
        w_store(n).start()
        return 0

    def run(step, begin, end):
        lax.fori_loop(begin, end, step, 0)

    def core_copy(u):
        return remote(pbuf.at[u, 1 - k], cbuf.at[u], csend.at[u], crecv.at[u], other)

    def source_of(u):
        dz, pp = SHARDS[u // 2]
        p_ = 1 - p if pp else p
        return lax.rem(y + 8 - z - dz, 4), p_

    low, high = pl.ds(0, 16), pl.ds(16, 16)

    def y_copy(u, side, part, number, to):
        return remote(
            sbuf.at[u, part, :], ybuf.at[u, side, part, :], ysend.at[u, number],
            yrecv.at[u, side, 0 if part is low else 1], to,
        )

    def y_wait(u, side, part):
        ref = ybuf.at[u, side, part, :]
        remote(ref, ref, ysend.at[u, 0], yrecv.at[u, side, 0 if part is low else 1], y_up).wait_recv()

    def stage1(u):
        core_copy(u).wait_recv()
        sbuf[u] = (pbuf[u, k].astype(F32) + cbuf[u].astype(F32)).astype(BF)
        away, _ = source_of(u)

        @pl.when(away == 2)
        def _():
            y_copy(u, 0, low, 0, y_up).start()
            y_copy(u, 1, high, 1, y_down).start()

        @pl.when(away == 3)
        def _():
            y_copy(u, 0, high, 0, y_up).start()

        @pl.when(away == 1)
        def _():
            y_copy(u, 1, low, 0, y_down).start()

    def stage2(u):
        away, _ = source_of(u)

        @pl.when(away == 3)
        def _():
            y_wait(u, 0, low)
            sbuf[u, low, :] = (sbuf[u, low, :].astype(F32) + ybuf[u, 0, low, :].astype(F32)).astype(BF)
            y_copy(u, 0, low, 1, y_up).start()

        @pl.when(away == 1)
        def _():
            y_wait(u, 1, high)
            sbuf[u, high, :] = (sbuf[u, high, :].astype(F32) + ybuf[u, 1, high, :].astype(F32)).astype(BF)
            y_copy(u, 1, high, 1, y_down).start()

    def x_copy(h):
        return remote(obuf.at[h], xbuf.at[h], xsend.at[h], xrecv.at[h], x_far)

    def stage3(u):
        away, p_ = source_of(u)
        h = u % 2

        @pl.when(away == 0)
        def _():
            for side in range(2):
                for part in (low, high):
                    y_wait(u, side, part)
            total = sbuf[u].astype(F32) + ybuf[u, 0].astype(F32) + ybuf[u, 1].astype(F32)

            where = [(h, slice(None))] if u // 2 < LAST else [(e, pl.ds(16 * h, 16)) for e in range(2)]
            size = 32 // len(where)

            @pl.when(p_ == q)
            def _():
                for e, (i, rows) in enumerate(where):
                    fbuf[i, rows, :] = total[size * e : size * e + size]

            @pl.when(p_ != q)
            def _():
                for e, (i, rows) in enumerate(where):
                    obuf[i, rows, :] = total[size * e : size * e + size].astype(BF)
                for i, rows in where:
                    remote(obuf.at[i, rows, :], xbuf.at[i, rows, :], xsend.at[h], xrecv.at[h], x_far).start()

    def units(*shards):
        return [2 * s + h for s in shards for h in range(2)]

    def turn_tokens(i, _):
        part = strip_of(i)
        for s in range(8):
            value = tbuf[pl.ds(first_of(*SHARDS[s]), 2), :, part].reshape(128, BLOCK)
            (tt_early if s < 4 else tt_late)[part, pl.ds(128 * (s % 4), 128)] = value.T
        return 0

    own_g.wait()
    partial_sums(whole_shards(0))

    g_wait(ZM + 1, 32, 1, 0)
    g_send(RM, 32, 1, 0, z_down)
    g_wait(XN + 0, 0, 0, 1)
    for j in range(2):
        g_send(BP + j, 16 * j, 0, 1, z_up, size=16)
    g_wait(ZP + 1, 32, 3, 0)
    g_send(XX + 0, 32, 3, 0, x_near)
    t_wait(TX, 0, 1)
    t_send(TYP + 1, 0, 1, y_up)
    t_send(TYM + 1, 0, 1, y_down)
    t_share(0, 1)
    early = ((1, (1,)), (2, (1,)), (3, (0,)))
    partial_sums(early)
    for u in units(0):
        stage1(u)
    t_wait(TYP, 3, 0)
    t_send(TRP, 3, 0, y_up)
    t_share(3, 0)
    t_wait(TYM, 1, 0)
    t_share(1, 0)

    g_wait(ZP + 0, 0, 3, 0)
    g_send(RP, 0, 3, 0, z_up)
    g_wait(ZM + 0, 0, 1, 0)
    g_send(XX + 1, 0, 1, 0, x_near)
    t_wait(TYM + 1, 1, 1)
    t_send(TRM, 1, 1, y_down)
    t_share(1, 1)
    t_wait(TYP + 1, 3, 1)
    t_share(3, 1)
    for u in (3, 5, 6):
        stage1(u)
    for u in units(0):
        stage2(u)
    g_wait(XN + 1, 32, 0, 1)
    for j in range(2):
        g_send(BM + j, 32 + 16 * j, 0, 1, z_down, size=16)
    g_wait(BP + 0, 0, 3, 1, 16)
    g_send(CP + 0, 0, 3, 1, z_up, size=16)
    partial_sums(((1, (0,)), (2, (0,)), (3, (1,))))
    g_wait(BP + 1, 16, 3, 1, 16)
    g_send(CP + 1, 16, 3, 1, z_up, size=16)

    t_wait(TRP, 2, 0)
    t_share(2, 0)
    t_wait(TRM, 2, 1)
    t_share(2, 1)
    own_t.wait()
    for n in range(8):
        ref = t_slot(n // 2, n % 2, 1 - k)
        remote(ref, ref, tcsend.at[n], tcrecv.at[n], other).wait_recv()
    run(turn_tokens, 0, blocks)

    for u in (3, 5, 6):
        stage2(u)
    for u in (2, 4, 7):
        stage1(u)
    run(first_pass, 0, 4)
    g_wait(BM + 0, 32, 1, 1, 16)
    g_send(CM + 0, 32, 1, 1, z_down, size=16)
    g_wait(XX + 0, 32, 3, 1)
    partial_sums(whole_shards(4))
    for u in units(0):
        stage3(u)
    for u in (2, 4, 7):
        stage2(u)
    g_wait(BM + 1, 48, 1, 1, 16)
    g_send(CM + 1, 48, 1, 1, z_down, size=16)
    run(first_pass, 4, 8)
    for u in units(4):
        stage1(u)
    g_wait(RM, 32, 2, 0)
    g_wait(RP, 0, 2, 0)
    partial_sums(whole_shards(5))
    for u in units(1, 2, 3):
        stage3(u)
    run(first_pass, 8, strips)
    for u in units(4):
        stage2(u)
    for u in units(5):
        stage1(u)
    g_wait(XX + 1, 0, 1, 1)
    g_wait(CP + 0, 0, 2, 1, 16)
    g_wait(CM + 0, 32, 2, 1, 16)
    partial_sums([(6, (0, 1)), (7, (0,))])
    for u in units(5):
        stage2(u)
    for u in units(4):
        stage3(u)
    for u in (12, 13, 14):
        stage1(u)
    g_wait(CP + 1, 16, 2, 1, 16)
    g_wait(CM + 1, 48, 2, 1, 16)
    partial_sums([(7, (1,))])
    for u in (12, 13, 14):
        stage2(u)
    for u in units(5):
        stage3(u)
    run(last_pass, 0, 2)
    stage1(15)
    for u in units(6):
        stage3(u)
    run(last_pass, 2, 5)
    stage2(15)
    stage3(14)
    run(last_pass, 5, 9)
    stage3(15)
    run(last_pass, 9, strips)

    for h in range(2):
        x_copy(h).wait_recv()
    for h in range(2):
        x_copy(h).wait_send()
    obuf[...] = (fbuf[...] + xbuf[...].astype(F32)).astype(BF)
    i_store = pltpu.make_async_copy(obuf, ig_out, iosem)
    i_store.start()

    for kind in range(G_COPIES):
        size = 16 if kind >= BP else 32
        ref = piece(0, 0, 0, size)
        remote(ref, ref, gsend.at[kind], grecv.at[kind], z_up).wait_send()
    for kind in range(7):
        ref = t_slot(0, 0)
        remote(ref, ref, tsend.at[kind], trecv.at[kind], y_up).wait_send()
    for n in range(8):
        ref = t_slot(0, 0)
        remote(ref, ref, tcsend.at[n], tcrecv.at[n], other).wait_send()
    for u in range(16):
        core_copy(u).wait_send()
        away, _ = source_of(u)

        @pl.when(away != 0)
        def _():
            y_copy(u, 0, low, 0, y_up).wait_send()
            y_copy(u, 0, low, 1, y_up).wait_send()

    for n in range(strips - 3, strips):
        w_store(n).wait()
    i_store.wait()


def main_call(tokens, out_grad, weight, block_mask):
    d, ff = weight.shape
    vmem, whole, dma = pltpu.VMEM, pl.BlockSpec(memory_space=pl.ANY), pltpu.SemaphoreType.DMA
    return pl.pallas_call(
        main_kernel,
        out_shape=(jax.ShapeDtypeStruct((2, 32, d), BF), jax.ShapeDtypeStruct((d, ff), BF)),
        in_specs=[pl.BlockSpec(memory_space=pltpu.SMEM), whole, whole, whole],
        out_specs=(whole, whole),
        scratch_shapes=[
            vmem((16, 64, ff), BF),
            vmem((16, 64, d), BF),
            vmem((2, BLOCK, ff), BF),
            vmem((ff, d), BF),
            vmem((d, 512), BF),
            vmem((d, 512), BF),
            vmem((ff // BLOCK, d, BLOCK), F32),
            vmem((3, d, BLOCK), BF),
            vmem((16, 2, 32, d), BF),
            vmem((16, 32, d), BF),
            vmem((16, 32, d), BF),
            vmem((16, 2, 32, d), BF),
            vmem((2, 32, d), BF),
            vmem((2, 32, d), F32),
            vmem((2, 32, d), BF),
            dma((G_COPIES,)), dma((G_COPIES,)), dma((7,)), dma((7,)), dma((8,)), dma((8,)),
            dma((16,)), dma((16,)), dma((16, 2)), dma((16, 2, 2)), dma((2,)), dma((2,)),
            dma((d // BLOCK,)), dma((2,)), dma((3,)), dma,
        ],
        compiler_params=pltpu.CompilerParams(
            collective_id=0, has_side_effects=True, vmem_limit_bytes=60 * 1024 * 1024
        ),
        name="gather_and_grads",
    )(block_mask, tokens, out_grad.reshape(2, 64, ff), weight)


def keep_kernel(mask, ig_in, full, ig_out, wg, igv, rows, isem, insem, outsem):
    blocks, strips = wg.shape[0] // BLOCK, wg.shape[1] // BLOCK
    i_load = pltpu.make_async_copy(ig_in, igv, isem.at[0])
    i_save = pltpu.make_async_copy(igv, ig_out, isem.at[1])

    def load(i, j):
        at = (pl.ds(i * BLOCK, BLOCK), pl.ds(pl.multiple_of(j * BLOCK, BLOCK), BLOCK))
        return pltpu.make_async_copy(full.at[at[0], at[1]], rows.at[i, :, at[1]], insem.at[i, j])

    def save(i):
        return pltpu.make_async_copy(rows.at[i], wg.at[pl.ds(i * BLOCK, BLOCK), :], outsem.at[i])

    for i in range(blocks):
        def begin(j, _, i=i):
            @pl.when(mask[i, j] != 0)
            def _():
                load(i, j).start()

            return 0

        lax.fori_loop(0, strips, begin, 0)
    i_load.start()
    for i in range(blocks):
        def end(j, _, i=i):
            @pl.when(mask[i, j] == 0)
            def _():
                rows[i, :, pl.ds(pl.multiple_of(j * BLOCK, BLOCK), BLOCK)] = jnp.zeros((BLOCK, BLOCK), BF)

            @pl.when(mask[i, j] != 0)
            def _():
                load(i, j).wait()

            return 0

        lax.fori_loop(0, strips, end, 0)
        save(i).start()
    i_load.wait()
    i_save.start()
    for i in range(blocks):
        save(i).wait()
    i_save.wait()


def keep_call(block_mask, input_grad, full):
    d, ff = full.shape
    whole, dma = pl.BlockSpec(memory_space=pl.ANY), pltpu.SemaphoreType.DMA
    return pl.pallas_call(
        keep_kernel,
        out_shape=(jax.ShapeDtypeStruct(input_grad.shape, BF), jax.ShapeDtypeStruct((d, ff), BF)),
        in_specs=[pl.BlockSpec(memory_space=pltpu.SMEM), whole, whole],
        out_specs=(whole, whole),
        scratch_shapes=[
            pltpu.VMEM(input_grad.shape, BF),
            pltpu.VMEM((d // BLOCK, BLOCK, ff), BF),
            dma((2,)), dma((d // BLOCK, ff // BLOCK)), dma((d // BLOCK,)),
        ],
        compiler_params=pltpu.CompilerParams(vmem_limit_bytes=60 * 1024 * 1024),
        name="keep_blocks",
    )(block_mask, input_grad, full)


def local(tokens, out_grad, weight, block_mask):
    input_grad, full = main_call(tokens, out_grad, weight, block_mask)
    return keep_call(block_mask, input_grad.reshape(64, weight.shape[0]), full)


def solution(mesh):
    in_specs = (P("col", "row"), P("row", "col"), P("row", "col"), P("row", "col"))
    out_specs = (P("col", "row"), P("row", "col"))
    return jax.shard_map(local, mesh=mesh, in_specs=in_specs, out_specs=out_specs, check_vma=False)
```

```python
import jax
import jax.numpy as jnp
from jax import lax
from jax.experimental import pallas as pl
from jax.experimental.pallas import tpu as pltpu
from jax.sharding import PartitionSpec as P

BLOCK = 256
MESH = pl.DeviceIdType.MESH
BF = jnp.bfloat16
F32 = jnp.float32

SHARDS = ((0, 0), (1, 0), (3, 0), (0, 1), (3, 1), (2, 0), (1, 1), (2, 1))
LAST = 7
PART = 128
MAIN_VMEM = 53 * 1024 * 1024 + 512 * 1024
ZP, ZM, XN, XX, RP, RM, BP, BM, CP, CM = 0, 2, 4, 6, 8, 9, 10, 12, 14, 16
G_COPIES = 18
TX, TYP, TYM, TRP, TRM = 0, 1, 3, 5, 6


def main_kernel(
    mask, tok, og, w, ig_out, wg_out,
    gbuf, tbuf, wbuf, wt, tt_early, tt_late, acc, pbuf, cbuf, sbuf, ybuf, xbuf, fbuf, obuf,
    gsend, grecv, tsend, trecv, tcsend, tcrecv, csend, crecv, ysend, yrecv, xsend, xrecv,
    wsem, lsem, iosem,
):
    row, col = lax.axis_index("row"), lax.axis_index("col")
    z, p = lax.div(row, 2), lax.rem(row, 2)
    y, q, k = lax.div(col, 4), lax.rem(lax.div(col, 2), 2), lax.rem(col, 2)

    def ring(v, step):
        return lax.rem(v + step, 4)

    def device(z_=z, p_=p, y_=y, q_=q, k_=k):
        return (2 * z_ + p_, 4 * y_ + 2 * q_ + k_)

    z_up, z_down = device(z_=ring(z, 1)), device(z_=ring(z, 3))
    x_near = device(p_=1 - p)
    y_up, y_down = device(y_=ring(y, 1)), device(y_=ring(y, 3))
    x_far, other = device(q_=1 - q), device(k_=1 - k)

    def remote(src, dst, send, recv, to):
        return pltpu.make_async_remote_copy(
            src_ref=src, dst_ref=dst, send_sem=send, recv_sem=recv, device_id=to, device_id_type=MESH
        )

    def first_of(dz, pp):
        return 4 * ring(z, dz) + 2 * (1 - p if pp else p)

    def piece(dz, pp, start, size=32):
        return gbuf.at[pl.ds(first_of(dz, pp), 2), pl.ds(start, size), :]

    def g_send(kind, start, dz, pp, to, src=None, size=32):
        ref = piece(dz, pp, start, size)
        remote(ref if src is None else src, ref, gsend.at[kind], grecv.at[kind], to).start()

    def g_wait(kind, start, dz, pp, size=32):
        ref = piece(dz, pp, start, size)
        remote(ref, ref, gsend.at[kind], grecv.at[kind], z_up).wait_recv()

    def t_slot(dy, qq, k_=k):
        q_ = 1 - q if qq else q
        return tbuf.at[4 * ring(y, dy) + 2 * q_ + k_]

    def t_send(kind, dy, qq, to, src=None):
        ref = t_slot(dy, qq)
        remote(ref if src is None else src, ref, tsend.at[kind], trecv.at[kind], to).start()

    def t_wait(kind, dy, qq):
        ref = t_slot(dy, qq)
        remote(ref, ref, tsend.at[kind], trecv.at[kind], y_up).wait_recv()

    def t_share(dy, qq, src=None):
        ref = t_slot(dy, qq)
        n = 2 * dy + qq
        remote(ref if src is None else src, ref, tcsend.at[n], tcrecv.at[n], other).start()

    blocks = wt.shape[1] // BLOCK
    strips = wt.shape[0] // BLOCK

    def w_load(i):
        return pltpu.make_async_copy(w.at[pl.ds(i * PART, PART), :], wbuf.at[i % 2], wsem.at[i])

    own_g = pltpu.make_async_copy(og, gbuf.at[pl.ds(4 * z + 2 * p, 2)], lsem.at[0])
    own_t = pltpu.make_async_copy(tok, t_slot(0, 0), lsem.at[1])
    own_g.start()
    w_load(0).start()
    w_load(1).start()
    own_t.start()

    barrier = pltpu.get_barrier_semaphore()
    peers = (z_up, z_down, x_near, y_up, y_down, x_far, other)
    for peer in peers:
        pl.semaphore_signal(barrier, inc=1, device_id=peer, device_id_type=MESH)
    pl.semaphore_wait(barrier, len(peers))

    def half_of_own(h):
        return og.at[:, pl.ds(32 * h, 32), :]

    g_send(ZP + 1, 32, 0, 0, z_up, half_of_own(1))
    g_send(ZM + 1, 32, 0, 0, z_down, half_of_own(1))
    g_send(XN + 0, 0, 0, 0, x_near, half_of_own(0))
    t_send(TX, 0, 0, x_far, tok)
    g_send(ZP + 0, 0, 0, 0, z_up, half_of_own(0))
    g_send(ZM + 0, 0, 0, 0, z_down, half_of_own(0))
    g_send(XN + 1, 32, 0, 0, x_near, half_of_own(1))
    t_send(TYP, 0, 0, y_up, tok)
    t_send(TYM, 0, 0, y_down, tok)
    t_share(0, 0, tok)

    parts = wt.shape[1] // PART
    for i in range(parts):
        w_load(i).wait()

        def turn(j, _, i=i):
            cols = pl.ds(pl.multiple_of(j * BLOCK, BLOCK), BLOCK)
            keep = mask[i * PART // BLOCK, j].astype(F32).astype(BF)
            wt[cols, pl.ds(i * PART, PART)] = (wbuf[i % 2, :, cols] * keep).T
            return 0

        lax.fori_loop(0, strips, turn, 0)
        if i + 2 < parts:
            w_load(i + 2).start()

    def g_rows(items, part):
        values = []
        for s, halves in items:
            first = first_of(*SHARDS[s])
            if len(halves) == 2:
                value = gbuf[pl.ds(first, 2), :, part]
            elif s < LAST:
                value = gbuf[pl.ds(first, 2), pl.ds(32 * halves[0], 32), part]
            else:
                value = gbuf[pl.ds(first, 2), pl.ds(16 * halves[0], 16), part]
                values.append(value.reshape(32, value.shape[2]))
                value = gbuf[pl.ds(first, 2), pl.ds(16 * halves[0] + 32, 16), part]
            values.append(value.reshape(value.shape[0] * value.shape[1], value.shape[2]))
        return values[0] if len(values) == 1 else jnp.concatenate(values, axis=0)

    def whole_shards(*shards):
        return [(s, (0, 1)) for s in shards]

    def partial_sums(items):
        def step(n, _):
            part = pl.ds(pl.multiple_of(n * BLOCK, BLOCK), BLOCK)
            out = jnp.dot(g_rows(items, slice(None)), wt[:, part], preferred_element_type=F32).astype(BF)
            row = 0
            for s, halves in items:
                if s == LAST:
                    for e in range(2):
                        for c in range(2):
                            pbuf[2 * s + halves[0], c, pl.ds(16 * e, 16), part] = out[row : row + 16]
                            row += 16
                    continue
                for c in range(2):
                    for h in halves:
                        pbuf[2 * s + h, c, :, part] = out[row : row + 32]
                        row += 32
            return 0

        lax.fori_loop(0, blocks, step, 0)
        for s, halves in items:
            for h in halves:
                core_copy(2 * s + h).start()

    def strip_of(n):
        return pl.ds(pl.multiple_of(n * BLOCK, BLOCK), BLOCK)

    def first_pass(n, _):
        acc[n] = jnp.dot(tt_early[...], g_rows(whole_shards(0, 1, 2, 3), strip_of(n)), preferred_element_type=F32)
        return 0

    def last_pass(n, _):
        total = acc[n] + jnp.dot(
            tt_late[...], g_rows(whole_shards(4, 5, 6, 7), strip_of(n)), preferred_element_type=F32
        )
        wg_out[:, strip_of(n)] = total.astype(BF)
        return 0

    def run(step, begin, end):
        lax.fori_loop(begin, end, step, 0)

    def core_copy(u):
        return remote(pbuf.at[u, 1 - k], cbuf.at[u], csend.at[u], crecv.at[u], other)

    def source_of(u):
        dz, pp = SHARDS[u // 2]
        p_ = 1 - p if pp else p
        return lax.rem(y + 8 - z - dz, 4), p_

    low, high = pl.ds(0, 16), pl.ds(16, 16)

    def y_copy(u, side, part, number, to):
        return remote(
            sbuf.at[u, part, :], ybuf.at[u, side, part, :], ysend.at[u, number],
            yrecv.at[u, side, 0 if part is low else 1], to,
        )

    def y_wait(u, side, part):
        ref = ybuf.at[u, side, part, :]
        remote(ref, ref, ysend.at[u, 0], yrecv.at[u, side, 0 if part is low else 1], y_up).wait_recv()

    def stage1(u):
        core_copy(u).wait_recv()
        sbuf[u] = (pbuf[u, k].astype(F32) + cbuf[u].astype(F32)).astype(BF)
        away, _ = source_of(u)

        @pl.when(away == 2)
        def _():
            y_copy(u, 0, low, 0, y_up).start()
            y_copy(u, 1, high, 1, y_down).start()

        @pl.when(away == 3)
        def _():
            y_copy(u, 0, high, 0, y_up).start()

        @pl.when(away == 1)
        def _():
            y_copy(u, 1, low, 0, y_down).start()

    def stage2(u):
        away, _ = source_of(u)

        @pl.when(away == 3)
        def _():
            y_wait(u, 0, low)
            sbuf[u, low, :] = (sbuf[u, low, :].astype(F32) + ybuf[u, 0, low, :].astype(F32)).astype(BF)
            y_copy(u, 0, low, 1, y_up).start()

        @pl.when(away == 1)
        def _():
            y_wait(u, 1, high)
            sbuf[u, high, :] = (sbuf[u, high, :].astype(F32) + ybuf[u, 1, high, :].astype(F32)).astype(BF)
            y_copy(u, 1, high, 1, y_down).start()

    def x_copy(h):
        return remote(obuf.at[h], xbuf.at[h], xsend.at[h], xrecv.at[h], x_far)

    def stage3(u):
        away, p_ = source_of(u)
        h = u % 2

        @pl.when(away == 0)
        def _():
            for side in range(2):
                for part in (low, high):
                    y_wait(u, side, part)
            total = sbuf[u].astype(F32) + ybuf[u, 0].astype(F32) + ybuf[u, 1].astype(F32)

            where = [(h, slice(None))] if u // 2 < LAST else [(e, pl.ds(16 * h, 16)) for e in range(2)]
            size = 32 // len(where)

            @pl.when(p_ == q)
            def _():
                for e, (i, rows) in enumerate(where):
                    fbuf[i, rows, :] = total[size * e : size * e + size]

            @pl.when(p_ != q)
            def _():
                for e, (i, rows) in enumerate(where):
                    obuf[i, rows, :] = total[size * e : size * e + size].astype(BF)
                for i, rows in where:
                    remote(obuf.at[i, rows, :], xbuf.at[i, rows, :], xsend.at[h], xrecv.at[h], x_far).start()

    def units(*shards):
        return [2 * s + h for s in shards for h in range(2)]

    def turn_tokens(i, _):
        part = strip_of(i)
        for s in range(8):
            value = tbuf[pl.ds(first_of(*SHARDS[s]), 2), :, part].reshape(128, BLOCK)
            (tt_early if s < 4 else tt_late)[part, pl.ds(128 * (s % 4), 128)] = value.T
        return 0

    own_g.wait()
    partial_sums(whole_shards(0))

    g_wait(ZM + 1, 32, 1, 0)
    g_send(RM, 32, 1, 0, z_down)
    g_wait(XN + 0, 0, 0, 1)
    for j in range(2):
        g_send(BP + j, 16 * j, 0, 1, z_up, size=16)
    g_wait(ZP + 1, 32, 3, 0)
    g_send(XX + 0, 32, 3, 0, x_near)
    t_wait(TX, 0, 1)
    t_send(TYP + 1, 0, 1, y_up)
    t_send(TYM + 1, 0, 1, y_down)
    t_share(0, 1)
    early = ((1, (1,)), (2, (1,)), (3, (0,)))
    partial_sums(early)
    for u in units(0):
        stage1(u)
    t_wait(TYP, 3, 0)
    t_send(TRP, 3, 0, y_up)
    t_share(3, 0)
    t_wait(TYM, 1, 0)
    t_share(1, 0)

    g_wait(ZP + 0, 0, 3, 0)
    g_send(RP, 0, 3, 0, z_up)
    g_wait(ZM + 0, 0, 1, 0)
    g_send(XX + 1, 0, 1, 0, x_near)
    t_wait(TYM + 1, 1, 1)
    t_send(TRM, 1, 1, y_down)
    t_share(1, 1)
    t_wait(TYP + 1, 3, 1)
    t_share(3, 1)
    for u in (3, 5, 6):
        stage1(u)
    for u in units(0):
        stage2(u)
    g_wait(XN + 1, 32, 0, 1)
    for j in range(2):
        g_send(BM + j, 32 + 16 * j, 0, 1, z_down, size=16)
    g_wait(BP + 0, 0, 3, 1, 16)
    g_send(CP + 0, 0, 3, 1, z_up, size=16)
    partial_sums(((1, (0,)), (2, (0,)), (3, (1,))))
    g_wait(BP + 1, 16, 3, 1, 16)
    g_send(CP + 1, 16, 3, 1, z_up, size=16)

    t_wait(TRP, 2, 0)
    t_share(2, 0)
    t_wait(TRM, 2, 1)
    t_share(2, 1)
    own_t.wait()
    for n in range(8):
        ref = t_slot(n // 2, n % 2, 1 - k)
        remote(ref, ref, tcsend.at[n], tcrecv.at[n], other).wait_recv()
    run(turn_tokens, 0, blocks)

    for u in (3, 5, 6):
        stage2(u)
    for u in (2, 4, 7):
        stage1(u)
    run(first_pass, 0, 4)
    g_wait(BM + 0, 32, 1, 1, 16)
    g_send(CM + 0, 32, 1, 1, z_down, size=16)
    g_wait(XX + 0, 32, 3, 1)
    partial_sums(whole_shards(4))
    for u in units(0):
        stage3(u)
    for u in (2, 4, 7):
        stage2(u)
    g_wait(BM + 1, 48, 1, 1, 16)
    g_send(CM + 1, 48, 1, 1, z_down, size=16)
    run(first_pass, 4, 8)
    for u in units(4):
        stage1(u)
    g_wait(RM, 32, 2, 0)
    g_wait(RP, 0, 2, 0)
    partial_sums(whole_shards(5))
    for u in units(1, 2, 3):
        stage3(u)
    run(first_pass, 8, strips)
    for u in units(4):
        stage2(u)
    for u in units(5):
        stage1(u)
    g_wait(XX + 1, 0, 1, 1)
    g_wait(CP + 0, 0, 2, 1, 16)
    g_wait(CM + 0, 32, 2, 1, 16)
    partial_sums([(6, (0, 1)), (7, (0,))])
    for u in units(5):
        stage2(u)
    for u in units(4):
        stage3(u)
    for u in (12, 13, 14):
        stage1(u)
    g_wait(CP + 1, 16, 2, 1, 16)
    g_wait(CM + 1, 48, 2, 1, 16)
    partial_sums([(7, (1,))])
    for u in (12, 13, 14):
        stage2(u)
    for u in units(5):
        stage3(u)
    run(last_pass, 0, 2)
    stage1(15)
    for u in units(6):
        stage3(u)
    run(last_pass, 2, 5)
    stage2(15)
    stage3(14)
    run(last_pass, 5, 9)
    stage3(15)
    run(last_pass, 9, strips)

    for h in range(2):
        x_copy(h).wait_recv()
    for h in range(2):
        x_copy(h).wait_send()
    obuf[...] = (fbuf[...] + xbuf[...].astype(F32)).astype(BF)
    i_store = pltpu.make_async_copy(obuf, ig_out, iosem)
    i_store.start()

    for kind in range(G_COPIES):
        size = 16 if kind >= BP else 32
        ref = piece(0, 0, 0, size)
        remote(ref, ref, gsend.at[kind], grecv.at[kind], z_up).wait_send()
    for kind in range(7):
        ref = t_slot(0, 0)
        remote(ref, ref, tsend.at[kind], trecv.at[kind], y_up).wait_send()
    for n in range(8):
        ref = t_slot(0, 0)
        remote(ref, ref, tcsend.at[n], tcrecv.at[n], other).wait_send()
    for u in range(16):
        core_copy(u).wait_send()
        away, _ = source_of(u)

        @pl.when(away != 0)
        def _():
            y_copy(u, 0, low, 0, y_up).wait_send()
            y_copy(u, 0, low, 1, y_up).wait_send()

    i_store.wait()


def main_call(tokens, out_grad, weight, block_mask):
    d, ff = weight.shape
    vmem, whole, dma = pltpu.VMEM, pl.BlockSpec(memory_space=pl.ANY), pltpu.SemaphoreType.DMA
    return pl.pallas_call(
        main_kernel,
        out_shape=(jax.ShapeDtypeStruct((2, 32, d), BF), pltpu.VMEM((d, ff), BF)),
        in_specs=[pl.BlockSpec(memory_space=pltpu.SMEM), whole, whole, whole],
        out_specs=(whole, pl.BlockSpec(memory_space=pltpu.VMEM)),
        scratch_shapes=[
            vmem((16, 64, ff), BF),
            vmem((16, 64, d), BF),
            vmem((2, PART, ff), BF),
            vmem((ff, d), BF),
            vmem((d, 512), BF),
            vmem((d, 512), BF),
            vmem((ff // BLOCK, d, BLOCK), F32),
            vmem((16, 2, 32, d), BF),
            vmem((16, 32, d), BF),
            vmem((16, 32, d), BF),
            vmem((16, 2, 32, d), BF),
            vmem((2, 32, d), BF),
            vmem((2, 32, d), F32),
            vmem((2, 32, d), BF),
            dma((G_COPIES,)), dma((G_COPIES,)), dma((7,)), dma((7,)), dma((8,)), dma((8,)),
            dma((16,)), dma((16,)), dma((16, 2)), dma((16, 2, 2)), dma((2,)), dma((2,)),
            dma((d // PART,)), dma((2,)), dma,
        ],
        compiler_params=pltpu.CompilerParams(
            collective_id=0, has_side_effects=True, vmem_limit_bytes=MAIN_VMEM
        ),
        name="gather_and_grads",
    )(block_mask, tokens, out_grad.reshape(2, 64, ff), weight)


def keep_kernel(mask, ig_in, full, ig_out, wg, igv, zero, isem, outsem):
    blocks, strips = wg.shape[0] // BLOCK, wg.shape[1] // BLOCK
    i_load = pltpu.make_async_copy(ig_in, igv, isem.at[0])
    i_save = pltpu.make_async_copy(igv, ig_out, isem.at[1])
    i_load.start()
    zero[...] = jnp.zeros_like(zero)

    def place(i, j):
        return (pl.ds(i * BLOCK, BLOCK), pl.ds(pl.multiple_of(j * BLOCK, BLOCK), BLOCK))

    for i in range(blocks):
        def begin(j, _, i=i):
            at = place(i, j)

            @pl.when(mask[i, j] != 0)
            def _():
                pltpu.make_async_copy(full.at[at[0], at[1]], wg.at[at[0], at[1]], outsem.at[i]).start()

            @pl.when(mask[i, j] == 0)
            def _():
                pltpu.make_async_copy(zero, wg.at[at[0], at[1]], outsem.at[i]).start()

            return 0

        lax.fori_loop(0, strips, begin, 0)
    i_load.wait()
    i_save.start()
    for i in range(blocks):
        rows = pl.ds(i * BLOCK, BLOCK)
        pltpu.make_async_copy(full.at[rows, :], wg.at[rows, :], outsem.at[i]).wait()
    i_save.wait()


def keep_call(block_mask, input_grad, full):
    d, ff = full.shape
    whole, dma = pl.BlockSpec(memory_space=pl.ANY), pltpu.SemaphoreType.DMA
    return pl.pallas_call(
        keep_kernel,
        out_shape=(jax.ShapeDtypeStruct(input_grad.shape, BF), jax.ShapeDtypeStruct((d, ff), BF)),
        in_specs=[pl.BlockSpec(memory_space=pltpu.SMEM), whole, pl.BlockSpec(memory_space=pltpu.VMEM)],
        out_specs=(whole, whole),
        scratch_shapes=[
            pltpu.VMEM(input_grad.shape, BF),
            pltpu.VMEM((BLOCK, BLOCK), BF),
            dma((2,)), dma((d // BLOCK,)),
        ],
        compiler_params=pltpu.CompilerParams(vmem_limit_bytes=4 * 1024 * 1024),
        name="keep_blocks",
    )(block_mask, input_grad, full)


def local(tokens, out_grad, weight, block_mask):
    input_grad, full = main_call(tokens, out_grad, weight, block_mask)
    return keep_call(block_mask, input_grad.reshape(64, weight.shape[0]), full)


def solution(mesh):
    in_specs = (P("col", "row"), P("row", "col"), P("row", "col"), P("row", "col"))
    out_specs = (P("col", "row"), P("row", "col"))
    return jax.shard_map(local, mesh=mesh, in_specs=in_specs, out_specs=out_specs, check_vma=False)
```

```python
import jax
import jax.numpy as jnp
from jax import lax
from jax.experimental import pallas as pl
from jax.experimental.pallas import tpu as pltpu
from jax.sharding import PartitionSpec as P

BLOCK = 256
MESH = pl.DeviceIdType.MESH
BF = jnp.bfloat16
F32 = jnp.float32

SHARDS = ((0, 0), (1, 0), (3, 0), (0, 1), (3, 1), (2, 0), (1, 1), (2, 1))
LAST = 7
PART = 128
MAIN_VMEM = 53 * 1024 * 1024 + 512 * 1024
ZP, ZM, XN, XX, RP, RM, BP, BM, CP, CM = 0, 2, 4, 6, 8, 9, 10, 12, 14, 16
G_COPIES = 18
TX, TYP, TYM, TRP, TRM = 0, 1, 3, 5, 6


def main_kernel(
    mask, tok, og, w, ig_out, wg_out,
    gbuf, tbuf, wbuf, wt, tt_early, tt_late, acc, pbuf, cbuf, sbuf, ybuf, xbuf, fbuf, obuf,
    gsend, grecv, tsend, trecv, tcsend, tcrecv, csend, crecv, ysend, yrecv, xsend, xrecv,
    wsem, lsem, iosem,
):
    row, col = lax.axis_index("row"), lax.axis_index("col")
    z, p = lax.div(row, 2), lax.rem(row, 2)
    y, q, k = lax.div(col, 4), lax.rem(lax.div(col, 2), 2), lax.rem(col, 2)

    def ring(v, step):
        return lax.rem(v + step, 4)

    def device(z_=z, p_=p, y_=y, q_=q, k_=k):
        return (2 * z_ + p_, 4 * y_ + 2 * q_ + k_)

    z_up, z_down = device(z_=ring(z, 1)), device(z_=ring(z, 3))
    x_near = device(p_=1 - p)
    y_up, y_down = device(y_=ring(y, 1)), device(y_=ring(y, 3))
    x_far, other = device(q_=1 - q), device(k_=1 - k)

    def remote(src, dst, send, recv, to):
        return pltpu.make_async_remote_copy(
            src_ref=src, dst_ref=dst, send_sem=send, recv_sem=recv, device_id=to, device_id_type=MESH
        )

    def first_of(dz, pp):
        return 4 * ring(z, dz) + 2 * (1 - p if pp else p)

    def piece(dz, pp, start, size=32):
        return gbuf.at[pl.ds(first_of(dz, pp), 2), pl.ds(start, size), :]

    def g_send(kind, start, dz, pp, to, src=None, size=32):
        ref = piece(dz, pp, start, size)
        remote(ref if src is None else src, ref, gsend.at[kind], grecv.at[kind], to).start()

    def g_wait(kind, start, dz, pp, size=32):
        ref = piece(dz, pp, start, size)
        remote(ref, ref, gsend.at[kind], grecv.at[kind], z_up).wait_recv()

    def t_slot(dy, qq, k_=k):
        q_ = 1 - q if qq else q
        return tbuf.at[4 * ring(y, dy) + 2 * q_ + k_]

    def t_send(kind, dy, qq, to, src=None):
        ref = t_slot(dy, qq)
        remote(ref if src is None else src, ref, tsend.at[kind], trecv.at[kind], to).start()

    def t_wait(kind, dy, qq):
        ref = t_slot(dy, qq)
        remote(ref, ref, tsend.at[kind], trecv.at[kind], y_up).wait_recv()

    def t_share(dy, qq, src=None):
        ref = t_slot(dy, qq)
        n = 2 * dy + qq
        remote(ref if src is None else src, ref, tcsend.at[n], tcrecv.at[n], other).start()

    blocks = wt.shape[1] // BLOCK
    strips = wt.shape[0] // BLOCK

    def w_load(i):
        return pltpu.make_async_copy(w.at[pl.ds(i * PART, PART), :], wbuf.at[i % 2], wsem.at[i])

    own_g = pltpu.make_async_copy(og, gbuf.at[pl.ds(4 * z + 2 * p, 2)], lsem.at[0])
    own_t = pltpu.make_async_copy(tok, t_slot(0, 0), lsem.at[1])
    own_g.start()
    w_load(0).start()
    w_load(1).start()
    own_t.start()

    barrier = pltpu.get_barrier_semaphore()
    peers = (z_up, z_down, x_near, y_up, y_down, x_far, other)
    for peer in peers:
        pl.semaphore_signal(barrier, inc=1, device_id=peer, device_id_type=MESH)
    pl.semaphore_wait(barrier, len(peers))

    def half_of_own(h):
        return og.at[:, pl.ds(32 * h, 32), :]

    g_send(ZP + 1, 32, 0, 0, z_up, half_of_own(1))
    g_send(ZM + 1, 32, 0, 0, z_down, half_of_own(1))
    g_send(XN + 0, 0, 0, 0, x_near, half_of_own(0))
    t_send(TX, 0, 0, x_far, tok)
    g_send(ZP + 0, 0, 0, 0, z_up, half_of_own(0))
    g_send(ZM + 0, 0, 0, 0, z_down, half_of_own(0))
    g_send(XN + 1, 32, 0, 0, x_near, half_of_own(1))
    t_send(TYP, 0, 0, y_up, tok)
    t_send(TYM, 0, 0, y_down, tok)
    t_share(0, 0, tok)

    parts = wt.shape[1] // PART
    for i in range(parts):
        w_load(i).wait()

        def turn(j, _, i=i):
            cols = pl.ds(pl.multiple_of(j * BLOCK, BLOCK), BLOCK)
            keep = mask[i * PART // BLOCK, j].astype(F32).astype(BF)
            wt[cols, pl.ds(i * PART, PART)] = (wbuf[i % 2, :, cols] * keep).T
            return 0

        lax.fori_loop(0, strips, turn, 0)
        if i + 2 < parts:
            w_load(i + 2).start()

    def g_rows(items, part):
        values = []
        for s, halves in items:
            first = first_of(*SHARDS[s])
            if len(halves) == 2:
                value = gbuf[pl.ds(first, 2), :, part]
            elif s < LAST:
                value = gbuf[pl.ds(first, 2), pl.ds(32 * halves[0], 32), part]
            else:
                value = gbuf[pl.ds(first, 2), pl.ds(16 * halves[0], 16), part]
                values.append(value.reshape(32, value.shape[2]))
                value = gbuf[pl.ds(first, 2), pl.ds(16 * halves[0] + 32, 16), part]
            values.append(value.reshape(value.shape[0] * value.shape[1], value.shape[2]))
        return values[0] if len(values) == 1 else jnp.concatenate(values, axis=0)

    def whole_shards(*shards):
        return [(s, (0, 1)) for s in shards]

    def partial_sums(items):
        def step(n, _):
            part = pl.ds(pl.multiple_of(n * BLOCK, BLOCK), BLOCK)
            out = jnp.dot(g_rows(items, slice(None)), wt[:, part], preferred_element_type=F32).astype(BF)
            row = 0
            for s, halves in items:
                if s == LAST:
                    for e in range(2):
                        for c in range(2):
                            pbuf[2 * s + halves[0], c, pl.ds(16 * e, 16), part] = out[row : row + 16]
                            row += 16
                    continue
                for c in range(2):
                    for h in halves:
                        pbuf[2 * s + h, c, :, part] = out[row : row + 32]
                        row += 32
            return 0

        lax.fori_loop(0, blocks, step, 0)
        for s, halves in items:
            for h in halves:
                core_copy(2 * s + h).start()

    def strip_of(n):
        return pl.ds(pl.multiple_of(n * BLOCK, BLOCK), BLOCK)

    def first_pass(n, _):
        acc[n] = jnp.dot(tt_early[...], g_rows(whole_shards(0, 1, 2, 3), strip_of(n)), preferred_element_type=F32)
        return 0

    def last_pass(n, _):
        total = acc[n] + jnp.dot(
            tt_late[...], g_rows(whole_shards(4, 5, 6, 7), strip_of(n)), preferred_element_type=F32
        )
        wg_out[:, strip_of(n)] = total.astype(BF)
        return 0

    def run(step, begin, end):
        lax.fori_loop(begin, end, step, 0)

    def core_copy(u):
        return remote(pbuf.at[u, 1 - k], cbuf.at[u], csend.at[u], crecv.at[u], other)

    def source_of(u):
        dz, pp = SHARDS[u // 2]
        p_ = 1 - p if pp else p
        return lax.rem(y + 8 - z - dz, 4), p_

    low, high = pl.ds(0, 16), pl.ds(16, 16)

    def y_copy(u, side, part, number, to):
        return remote(
            sbuf.at[u, part, :], ybuf.at[u, side, part, :], ysend.at[u, number],
            yrecv.at[u, side, 0 if part is low else 1], to,
        )

    def y_wait(u, side, part):
        ref = ybuf.at[u, side, part, :]
        remote(ref, ref, ysend.at[u, 0], yrecv.at[u, side, 0 if part is low else 1], y_up).wait_recv()

    def stage1(u):
        core_copy(u).wait_recv()
        sbuf[u] = (pbuf[u, k].astype(F32) + cbuf[u].astype(F32)).astype(BF)
        away, _ = source_of(u)

        @pl.when(away == 2)
        def _():
            y_copy(u, 0, low, 0, y_up).start()
            y_copy(u, 1, high, 1, y_down).start()

        @pl.when(away == 3)
        def _():
            y_copy(u, 0, high, 0, y_up).start()

        @pl.when(away == 1)
        def _():
            y_copy(u, 1, low, 0, y_down).start()

    def stage2(u):
        away, _ = source_of(u)

        @pl.when(away == 3)
        def _():
            y_wait(u, 0, low)
            sbuf[u, low, :] = (sbuf[u, low, :].astype(F32) + ybuf[u, 0, low, :].astype(F32)).astype(BF)
            y_copy(u, 0, low, 1, y_up).start()

        @pl.when(away == 1)
        def _():
            y_wait(u, 1, high)
            sbuf[u, high, :] = (sbuf[u, high, :].astype(F32) + ybuf[u, 1, high, :].astype(F32)).astype(BF)
            y_copy(u, 1, high, 1, y_down).start()

    def x_copy(h):
        return remote(obuf.at[h], xbuf.at[h], xsend.at[h], xrecv.at[h], x_far)

    def stage3(u):
        away, p_ = source_of(u)
        h = u % 2

        @pl.when(away == 0)
        def _():
            for side in range(2):
                for part in (low, high):
                    y_wait(u, side, part)
            total = sbuf[u].astype(F32) + ybuf[u, 0].astype(F32) + ybuf[u, 1].astype(F32)

            where = [(h, slice(None))] if u // 2 < LAST else [(e, pl.ds(16 * h, 16)) for e in range(2)]
            size = 32 // len(where)

            @pl.when(p_ == q)
            def _():
                for e, (i, rows) in enumerate(where):
                    fbuf[i, rows, :] = total[size * e : size * e + size]

            @pl.when(p_ != q)
            def _():
                for e, (i, rows) in enumerate(where):
                    obuf[i, rows, :] = total[size * e : size * e + size].astype(BF)
                for i, rows in where:
                    remote(obuf.at[i, rows, :], xbuf.at[i, rows, :], xsend.at[h], xrecv.at[h], x_far).start()

    def units(*shards):
        return [2 * s + h for s in shards for h in range(2)]

    def turn_tokens(i, _):
        part = strip_of(i)
        for s in range(8):
            value = tbuf[pl.ds(first_of(*SHARDS[s]), 2), :, part].reshape(128, BLOCK)
            (tt_early if s < 4 else tt_late)[part, pl.ds(128 * (s % 4), 128)] = value.T
        return 0

    own_g.wait()
    partial_sums(whole_shards(0))

    g_wait(ZM + 1, 32, 1, 0)
    g_send(RM, 32, 1, 0, z_down)
    g_wait(XN + 0, 0, 0, 1)
    for j in range(2):
        g_send(BP + j, 16 * j, 0, 1, z_up, size=16)
    g_wait(ZP + 1, 32, 3, 0)
    g_send(XX + 0, 32, 3, 0, x_near)
    t_wait(TX, 0, 1)
    t_send(TYP + 1, 0, 1, y_up)
    t_send(TYM + 1, 0, 1, y_down)
    t_share(0, 1)
    early = ((1, (1,)), (2, (1,)), (3, (0,)))
    partial_sums(early)
    for u in units(0):
        stage1(u)
    t_wait(TYP, 3, 0)
    t_send(TRP, 3, 0, y_up)
    t_share(3, 0)
    t_wait(TYM, 1, 0)
    t_share(1, 0)

    g_wait(ZP + 0, 0, 3, 0)
    g_send(RP, 0, 3, 0, z_up)
    g_wait(ZM + 0, 0, 1, 0)
    g_send(XX + 1, 0, 1, 0, x_near)
    t_wait(TYM + 1, 1, 1)
    t_send(TRM, 1, 1, y_down)
    t_share(1, 1)
    t_wait(TYP + 1, 3, 1)
    t_share(3, 1)
    for u in (3, 5, 6):
        stage1(u)
    for u in units(0):
        stage2(u)
    g_wait(XN + 1, 32, 0, 1)
    for j in range(2):
        g_send(BM + j, 32 + 16 * j, 0, 1, z_down, size=16)
    g_wait(BP + 0, 0, 3, 1, 16)
    g_send(CP + 0, 0, 3, 1, z_up, size=16)
    partial_sums(((1, (0,)), (2, (0,)), (3, (1,))))
    g_wait(BP + 1, 16, 3, 1, 16)
    g_send(CP + 1, 16, 3, 1, z_up, size=16)

    t_wait(TRP, 2, 0)
    t_share(2, 0)
    t_wait(TRM, 2, 1)
    t_share(2, 1)
    own_t.wait()
    for n in range(8):
        ref = t_slot(n // 2, n % 2, 1 - k)
        remote(ref, ref, tcsend.at[n], tcrecv.at[n], other).wait_recv()
    run(turn_tokens, 0, blocks)

    for u in (3, 5, 6):
        stage2(u)
    for u in (2, 4, 7):
        stage1(u)
    run(first_pass, 0, 4)
    g_wait(BM + 0, 32, 1, 1, 16)
    g_send(CM + 0, 32, 1, 1, z_down, size=16)
    g_wait(XX + 0, 32, 3, 1)
    partial_sums(whole_shards(4))
    for u in units(0):
        stage3(u)
    for u in (2, 4, 7):
        stage2(u)
    g_wait(BM + 1, 48, 1, 1, 16)
    g_send(CM + 1, 48, 1, 1, z_down, size=16)
    run(first_pass, 4, 8)
    for u in units(4):
        stage1(u)
    g_wait(RM, 32, 2, 0)
    g_wait(RP, 0, 2, 0)
    partial_sums(whole_shards(5))
    for u in units(1, 2, 3):
        stage3(u)
    for u in units(4):
        stage2(u)
    for u in units(5):
        stage1(u)
    g_wait(XX + 1, 0, 1, 1)
    g_wait(CP + 0, 0, 2, 1, 16)
    g_wait(CM + 0, 32, 2, 1, 16)
    partial_sums([(6, (0, 1)), (7, (0,))])
    for u in units(5):
        stage2(u)
    for u in units(4):
        stage3(u)
    for u in (12, 13, 14):
        stage1(u)
    g_wait(CP + 1, 16, 2, 1, 16)
    g_wait(CM + 1, 48, 2, 1, 16)
    partial_sums([(7, (1,))])
    for u in (12, 13, 14):
        stage2(u)
    for u in units(5):
        stage3(u)
    run(first_pass, 8, strips)
    stage1(15)
    for u in units(6):
        stage3(u)
    run(last_pass, 0, 3)
    stage2(15)
    stage3(14)
    run(last_pass, 3, 7)
    stage3(15)
    run(last_pass, 7, strips)

    for h in range(2):
        x_copy(h).wait_recv()
    for h in range(2):
        x_copy(h).wait_send()
    obuf[...] = (fbuf[...] + xbuf[...].astype(F32)).astype(BF)
    i_store = pltpu.make_async_copy(obuf, ig_out, iosem)
    i_store.start()

    for kind in range(G_COPIES):
        size = 16 if kind >= BP else 32
        ref = piece(0, 0, 0, size)
        remote(ref, ref, gsend.at[kind], grecv.at[kind], z_up).wait_send()
    for kind in range(7):
        ref = t_slot(0, 0)
        remote(ref, ref, tsend.at[kind], trecv.at[kind], y_up).wait_send()
    for n in range(8):
        ref = t_slot(0, 0)
        remote(ref, ref, tcsend.at[n], tcrecv.at[n], other).wait_send()
    for u in range(16):
        core_copy(u).wait_send()
        away, _ = source_of(u)

        @pl.when(away != 0)
        def _():
            y_copy(u, 0, low, 0, y_up).wait_send()
            y_copy(u, 0, low, 1, y_up).wait_send()

    i_store.wait()


def main_call(tokens, out_grad, weight, block_mask):
    d, ff = weight.shape
    vmem, whole, dma = pltpu.VMEM, pl.BlockSpec(memory_space=pl.ANY), pltpu.SemaphoreType.DMA
    return pl.pallas_call(
        main_kernel,
        out_shape=(jax.ShapeDtypeStruct((2, 32, d), BF), pltpu.VMEM((d, ff), BF)),
        in_specs=[pl.BlockSpec(memory_space=pltpu.SMEM), whole, whole, whole],
        out_specs=(whole, pl.BlockSpec(memory_space=pltpu.VMEM)),
        scratch_shapes=[
            vmem((16, 64, ff), BF),
            vmem((16, 64, d), BF),
            vmem((2, PART, ff), BF),
            vmem((ff, d), BF),
            vmem((d, 512), BF),
            vmem((d, 512), BF),
            vmem((ff // BLOCK, d, BLOCK), F32),
            vmem((16, 2, 32, d), BF),
            vmem((16, 32, d), BF),
            vmem((16, 32, d), BF),
            vmem((16, 2, 32, d), BF),
            vmem((2, 32, d), BF),
            vmem((2, 32, d), F32),
            vmem((2, 32, d), BF),
            dma((G_COPIES,)), dma((G_COPIES,)), dma((7,)), dma((7,)), dma((8,)), dma((8,)),
            dma((16,)), dma((16,)), dma((16, 2)), dma((16, 2, 2)), dma((2,)), dma((2,)),
            dma((d // PART,)), dma((2,)), dma,
        ],
        compiler_params=pltpu.CompilerParams(
            collective_id=0, has_side_effects=True, vmem_limit_bytes=MAIN_VMEM
        ),
        name="gather_and_grads",
    )(block_mask, tokens, out_grad.reshape(2, 64, ff), weight)


def keep_kernel(mask, ig_in, full, ig_out, wg, igv, zero, isem, outsem):
    blocks, strips = wg.shape[0] // BLOCK, wg.shape[1] // BLOCK
    i_load = pltpu.make_async_copy(ig_in, igv, isem.at[0])
    i_save = pltpu.make_async_copy(igv, ig_out, isem.at[1])
    i_load.start()
    zero[...] = jnp.zeros_like(zero)

    def place(i, j):
        return (pl.ds(i * BLOCK, BLOCK), pl.ds(pl.multiple_of(j * BLOCK, BLOCK), BLOCK))

    for i in range(blocks):
        def begin(j, _, i=i):
            at = place(i, j)

            @pl.when(mask[i, j] != 0)
            def _():
                pltpu.make_async_copy(full.at[at[0], at[1]], wg.at[at[0], at[1]], outsem.at[i]).start()

            @pl.when(mask[i, j] == 0)
            def _():
                pltpu.make_async_copy(zero, wg.at[at[0], at[1]], outsem.at[i]).start()

            return 0

        lax.fori_loop(0, strips, begin, 0)
    i_load.wait()
    i_save.start()
    for i in range(blocks):
        rows = pl.ds(i * BLOCK, BLOCK)
        pltpu.make_async_copy(full.at[rows, :], wg.at[rows, :], outsem.at[i]).wait()
    i_save.wait()


def keep_call(block_mask, input_grad, full):
    d, ff = full.shape
    whole, dma = pl.BlockSpec(memory_space=pl.ANY), pltpu.SemaphoreType.DMA
    return pl.pallas_call(
        keep_kernel,
        out_shape=(jax.ShapeDtypeStruct(input_grad.shape, BF), jax.ShapeDtypeStruct((d, ff), BF)),
        in_specs=[pl.BlockSpec(memory_space=pltpu.SMEM), whole, pl.BlockSpec(memory_space=pltpu.VMEM)],
        out_specs=(whole, whole),
        scratch_shapes=[
            pltpu.VMEM(input_grad.shape, BF),
            pltpu.VMEM((BLOCK, BLOCK), BF),
            dma((2,)), dma((d // BLOCK,)),
        ],
        compiler_params=pltpu.CompilerParams(vmem_limit_bytes=4 * 1024 * 1024),
        name="keep_blocks",
    )(block_mask, input_grad, full)


def local(tokens, out_grad, weight, block_mask):
    input_grad, full = main_call(tokens, out_grad, weight, block_mask)
    return keep_call(block_mask, input_grad.reshape(64, weight.shape[0]), full)


def solution(mesh):
    in_specs = (P("col", "row"), P("row", "col"), P("row", "col"), P("row", "col"))
    out_specs = (P("col", "row"), P("row", "col"))
    return jax.shard_map(local, mesh=mesh, in_specs=in_specs, out_specs=out_specs, check_vma=False)
```
